32 devices in a mesh: groups: 2 (over y), freq: 4 (over z), sub: 4 (over x, core).
Axes of the slice: x: 2, y: 2, z: 4, core: 2. Of those that a mesh axis runs over, the one named last changes fastest.
Arguments:
- wavenumbers: float32 [512, 300], replicated, may hold values from 1 to 20
- receiver_shapes: bfloat16 [512, 300], replicated, may hold values from -6 to 6
- source_shapes: bfloat16 [512, 4, 300], replicated, may hold values from -6 to 6
- mode_counts: int32 [512], replicated, may hold values from 64 to 300, as said below
- source_depths: int32 [32], P('groups'), parts along dimension 0, may hold values from 0 to 3
- source_ranges: float32 [32], P('groups'), parts along dimension 0, may hold values from 0 to 0.5
- sections: int32 [2048], P(('freq', 'sub')), may hold values from 0 to 511, as said below
- recorded: bfloat16 [2048, 4096], P(('freq', 'sub')), may hold values from -6 to 6
Outputs:
- scores: float32 [32, 512], P('groups', ('freq', 'sub')), parts along dimension 0
The draws below stay inside these ranges and needn't reach their ends.
There are 2 independent parts, one for each index of `groups`. The reference program is written for one: setup_inputs(seed, part) draws one part's arguments, and reference() takes and returns one part's arrays. A program takes and returns all parts, laid end to end along the dimension named above; an argument that names none is the same for every part. Nothing has to cross between parts.
Inputs may be any that keep to these rules, and one draw needn't show every extreme that they name: `mode_counts`: counts rise with the bin index: bin f holds within 16 of 64 + floor((236) f / 511) modes, clipped to the range; the first bin holds 64 and the last 300. `sections`: each section holds exactly 4 channels.
All inputs are finite; a program needn't handle non-finite values.
Results may differ from the reference program's by a relative error of at most 0.0068.
Values may be sent and summed in bfloat16 or wider, within the bound.
A program may use at most 64 MiB of HBM per device.

```python
import math
import jax
import jax.numpy as jnp
from jax import lax

F = 512
MMAX = 300
MMIN = 64
NT = 4096
R = 2048
SEC = 512
NZ = 4
S = 16
F0 = 256


def draw_mode_counts(key, part):
    bin_numbers = jnp.arange(F, dtype=jnp.int32)
    ramp = MMIN + (MMAX - MMIN) * bin_numbers // max(F - 1, 1)
    jitter = jax.random.randint(key, (F,), -16, 17, dtype=jnp.int32)
    counts = jnp.clip(ramp + jitter, MMIN, MMAX)
    return counts.at[0].set(MMIN).at[F - 1].set(MMAX).astype(jnp.int32)


def draw_source_depths(key, part):
    depths = jax.random.randint(jax.random.fold_in(key, 7), (S,), 0, NZ, dtype=jnp.int32)
    return depths.at[0].set(0).at[S - 1].set(NZ - 1).astype(jnp.int32)


def draw_sections(key, part):
    order = jax.random.permutation(jax.random.fold_in(key, 11), R)
    return (order % SEC).astype(jnp.int32)


def shard_levels(rng, shape, split, low, top_value):
    factor_of = 1.0
    for position, parts in split:
        steps = jax.random.uniform(jax.random.fold_in(jax.random.fold_in(rng, 6), position), (parts,), jnp.float32, low / len(split), top_value / len(split))
        factor_of = factor_of * jnp.repeat(jnp.exp(steps), shape[position] // parts).reshape((-1,) + (1,) * (len(shape) - 1 - position))
    return factor_of


def scatter_about(own_key, extent, deviation, reach, cuts=(), kind=jnp.bfloat16):
    values = deviation * jax.random.normal(own_key, extent, jnp.float32)
    if cuts:
        values = values * shard_levels(own_key, extent, cuts, -0.22, 0.18)
    return jnp.clip(values, -reach, reach).astype(kind)


def setup_inputs(seed: int = 0, part: int = 0) -> dict:
    key_list = jax.random.split(jax.random.key(seed), 9)
    part_keys = jax.random.split(jax.random.fold_in(key_list[8], part), 9)
    wavenumbers = jnp.clip(jax.random.uniform(key_list[0], (F, MMAX), jnp.float32, 1.0, 20.0), 1.0, 20.0)
    receiver_shapes = scatter_about(key_list[1], (F, MMAX), 1.0, 6.0)
    source_shapes = scatter_about(key_list[2], (F, NZ, MMAX), 1.0, 6.0)
    mode_counts = draw_mode_counts(jax.random.fold_in(key_list[8], 71), part)
    source_depths = draw_source_depths(jax.random.fold_in(jax.random.fold_in(key_list[8], part), 71), part)
    source_ranges = jnp.clip(jax.random.uniform(part_keys[5], (S,), jnp.float32, 0.0, 0.5), 0.0, 0.5)
    sections = draw_sections(jax.random.fold_in(key_list[8], 71), part)
    recorded = scatter_about(key_list[7], (R, NT), 1.0, 6.0, ((0, 16),))
    return dict(wavenumbers=wavenumbers, receiver_shapes=receiver_shapes, source_shapes=source_shapes, mode_counts=mode_counts, source_depths=source_depths, source_ranges=source_ranges, sections=sections, recorded=recorded)


def rounded(operand):
    return lax.optimization_barrier(operand.astype(jnp.bfloat16)).astype(jnp.float32)

def source_factor(wave_part, source_table, counts, depths, ranges):
    depth_grid = source_table.shape[1]
    mode_width = wave_part.shape[1]
    chooser = (depths[:, None] == jnp.arange(depth_grid, dtype=jnp.int32)[None, :]).astype(jnp.float32)
    at_source = jnp.einsum('sz,bzm->bsm', chooser, source_table.astype(jnp.float32), precision=lax.Precision.HIGHEST)
    mode_live = (jnp.arange(mode_width, dtype=jnp.int32)[None, :] < counts[:, None]).astype(jnp.float32)
    phases = wave_part[:, None, :] * ranges[None, :, None]
    weighted = at_source * mode_live[:, None, :]
    return jnp.concatenate([weighted * jnp.cos(phases), -weighted * jnp.sin(phases)], axis=2).astype(jnp.bfloat16)

def receiver_factor(wave_part, receiver_table, positions):
    mode_width = wave_part.shape[1]
    phases = wave_part[:, :, None] * positions[None, None, :]
    amplitude = receiver_table.astype(jnp.float32)[:, :, None] * 8.0 / jnp.sqrt(phases * mode_width)
    real_part = amplitude * jnp.cos(phases)
    imag_part = amplitude * jnp.sin(phases)
    upper_rows = jnp.concatenate([real_part, imag_part], axis=2)
    lower_rows = jnp.concatenate([-imag_part, real_part], axis=2)
    return jnp.concatenate([upper_rows, lower_rows], axis=1).astype(jnp.bfloat16)

def time_table(start_time, time_span):
    bin_numbers = F0 + jnp.arange(F, dtype=jnp.int32)
    sample_times = start_time + jnp.arange(time_span, dtype=jnp.int32)
    phase_turns = bin_numbers[:, None] * sample_times[None, :] % NT
    angles = phase_turns.astype(jnp.float32) * (2.0 * math.pi / NT)
    return jnp.stack([jnp.cos(angles), -jnp.sin(angles)], axis=1).astype(jnp.bfloat16)

def reference(wavenumbers, receiver_shapes, source_shapes, mode_counts, source_depths, source_ranges, sections, recorded):
    source_side = rounded(source_factor(wavenumbers, source_shapes, mode_counts, source_depths, source_ranges))
    dft_table = rounded(time_table(jnp.int32(0), NT))
    channel_block = R // 32

    def one_block(first_row):
        channel = first_row + jnp.arange(channel_block, dtype=jnp.int32)
        positions = 1.0 + 2.0 * channel.astype(jnp.float32) / R
        receiver_side = rounded(receiver_factor(wavenumbers, receiver_shapes, positions))
        spectra = rounded(jnp.einsum('fsk,fkn->fsn', source_side, receiver_side))
        spectra = spectra.reshape(F, S, 2, channel_block)
        series = jnp.einsum('fsqn,fqt->snt', spectra, dft_table) * (1.0 / math.sqrt(F))
        waveform = lax.dynamic_slice_in_dim(recorded, first_row, channel_block, 0).astype(jnp.float32)
        return lax.optimization_barrier(jnp.sum(jnp.tanh(series) * waveform[None, :, :], axis=2))
    first_rows = jnp.arange(32, dtype=jnp.int32) * channel_block
    correlation = lax.map(one_block, first_rows)
    correlation = jnp.transpose(correlation, (1, 0, 2)).reshape(S, R)
    member = (sections[:, None] == jnp.arange(SEC, dtype=jnp.int32)[None, :]).astype(jnp.float32)
    return jnp.dot(correlation, member, precision=lax.Precision.HIGHEST) * (1.0 / math.sqrt(NT * (R // SEC)))
```

```python
import functools
import math

import jax
import jax.numpy as jnp
import numpy as np
from jax import lax
from jax.experimental import pallas as pl
from jax.experimental.pallas import tpu as pltpu
from jax.sharding import PartitionSpec as P

MMIN = 64
F0 = 256
SPREAD = 16
K_LOW, K_TOP = 1.0, 20.0
R_TOP = 0.5
K_MID, K_HALF = 0.5 * (K_LOW + K_TOP), 0.5 * (K_TOP - K_LOW)
LANES = 128
TERMS = 16
TWO_PI = 2.0 * math.pi


def sincos_turns(turns):
    part = turns - jnp.floor(turns + 0.5)
    sq = part * part
    p2 = math.pi * math.pi
    s = jnp.full_like(part, -(p2**5) / math.factorial(11))
    for n in (9, 7, 5, 3, 1):
        s = s * sq + ((-1) ** ((n - 1) // 2)) * p2 ** ((n - 1) // 2) / math.factorial(n)
    s = s * (part * math.pi)
    c = jnp.full_like(part, p2**6 / math.factorial(12))
    for n in (10, 8, 6, 4, 2, 0):
        c = c * sq + ((-1) ** (n // 2)) * p2 ** (n // 2) / math.factorial(n)
    return 1.0 - 2.0 * s * s, 2.0 * s * c


def term_constants():
    nodes = np.cos(np.pi * (np.arange(TERMS) + 0.5) / TERMS)[: TERMS // 2]
    order = np.arange(TERMS)
    table = np.cos(order[:, None] * np.arccos(nodes)[None, :])
    table *= (np.where(order == 0, 1.0, 2.0) * 2.0 / TERMS)[:, None]
    half = TERMS // 2
    out = np.zeros((half, LANES), np.float32)
    out[:, 0] = K_HALF * nodes
    out[:, 1 : 1 + half] = table[0::2]
    out[:, 1 + half : 1 + 2 * half] = table[1::2]
    return out


def place_of(n):
    return n // 2 if n % 2 == 0 else TERMS // 2 + n // 2


def tile_groups(bins, modes, per_group):
    runs = []
    for group in range(bins // per_group):
        last = (group + 1) * per_group - 1
        top = min(modes, MMIN + (modes - MMIN) * last // max(bins - 1, 1) + SPREAD)
        tiles = -(-top // LANES)
        if runs and runs[-1][2] == tiles:
            runs[-1][1] = group + 1
        else:
            runs.append([group, group + 1, tiles])
    return runs


def replica_kernel(
    shape,
    depths_ref,
    place_ref,
    ranges_ref,
    consts_ref,
    wave_ref,
    ampl_ref,
    recorded_ref,
    out_ref,
    re_ref,
    im_ref,
    tab_ref,
    part_ref,
    psi_ref,
    coef_ref,
):
    bins, modes, depth_grid, sources, channels, samples, receivers = shape
    quarter = bins // 4
    span = samples // 4
    half = TERMS // 2
    first_x = place_ref[0]
    centre = place_ref[1]

    def modal(start, tiles):
        rows = pl.ds(pl.multiple_of(start, 8), 8)
        cols = pl.ds(0, tiles * LANES)
        wave = wave_ref[rows, cols]
        cosine, sine = sincos_turns(wave * (centre * (1.0 / TWO_PI)))
        xi = (wave - K_MID) * (1.0 / K_HALF)
        twice = xi + xi
        parts = []
        for z in range(depth_grid):
            ampl = ampl_ref[z, rows, cols]
            parts.append((ampl * cosine, ampl * sine))
        lane = lax.broadcasted_iota(jnp.int32, (8, LANES), 1)
        total = jnp.zeros((8, LANES), jnp.float32)
        before, now = None, None
        for n in range(TERMS):
            if n == 1:
                before, now = jnp.ones_like(xi), xi
            elif n > 1:
                before, now = now, twice * now - before
            for z in range(depth_grid):
                for c in range(2):
                    product = parts[z][c] if n == 0 else parts[z][c] * now
                    folded = product[:, :LANES]
                    for tile in range(1, tiles):
                        folded = folded + product[:, tile * LANES : (tile + 1) * LANES]
                    value = jnp.sum(folded, axis=1, keepdims=True)
                    at = z * 2 * TERMS + c * TERMS + place_of(n)
                    total = jnp.where(lane == at, value, total)
        real_lane = lane % (2 * TERMS) < TERMS
        swapped = jnp.where(
            real_lane, pltpu.roll(total, LANES - TERMS, 1), -pltpu.roll(total, TERMS, 1)
        )
        re_ref[rows, :] = total
        im_ref[rows, :] = swapped

    for first, last, tiles in tile_groups(bins, modes, 32):

        def body(i, carry, first=first, last=last, tiles=tiles):
            count = last - first
            modal((i // count) * quarter + (first + i % count) * 8, tiles)
            return carry

        lax.fori_loop(0, 4 * (last - first), body, 0)

    for r in range(4):
        row = lax.broadcasted_iota(jnp.int32, (quarter, LANES), 0)
        column = lax.broadcasted_iota(jnp.int32, (quarter, LANES), 1)
        number = F0 + 4 * row + r
        whole = (number * column) % samples
        cosine, sine = sincos_turns(whole.astype(jnp.float32) * (1.0 / samples))
        turn = (number * LANES) % samples
        step_c, step_s = sincos_turns(turn.astype(jnp.float32) * (1.0 / samples))
        for block in range(span // LANES):
            cols = slice(block * LANES, (block + 1) * LANES)
            tab_ref[:quarter, cols] = cosine.astype(jnp.bfloat16)
            tab_ref[quarter:, cols] = (-sine).astype(jnp.bfloat16)
            cosine, sine = cosine * step_c - sine * step_s, cosine * step_s + sine * step_c
        rows = slice(r * quarter, (r + 1) * quarter)
        left = jnp.concatenate([re_ref[rows, :].T, im_ref[rows, :].T], axis=1)
        part_ref[r] = jnp.dot(
            left.astype(jnp.bfloat16), tab_ref[...], preferred_element_type=jnp.float32
        )

    def times_i(value):
        blocks = []
        for z in range(depth_grid):
            base = z * 2 * TERMS
            blocks.append(-value[base + TERMS : base + 2 * TERMS])
            blocks.append(value[base : base + TERMS])
        return jnp.concatenate(blocks, axis=0)

    for block in range(span // LANES):
        cols = slice(block * LANES, (block + 1) * LANES)
        p0, p1, p2, p3 = (part_ref[r, :, cols] for r in range(4))
        even, odd = p0 + p2, p1 + p3
        gap, turned = p0 - p2, times_i(p1 - p3)
        for q, value in enumerate((even + odd, gap + turned, even - odd, gap - turned)):
            at = q * span + block * LANES
            psi_ref[:, at : at + LANES] = value.astype(jnp.bfloat16)

    channel = lax.broadcasted_iota(jnp.int32, (1, channels), 1).astype(jnp.float32)
    position = first_x + channel * (2.0 / receivers)
    spread = lax.rsqrt(position)
    nodes = consts_ref[:, 0:1]
    for s in range(sources):
        offset = position - (ranges_ref[s] + centre)
        cosine, sine = sincos_turns(nodes * offset * (1.0 / TWO_PI))
        even = jnp.zeros((half, channels), jnp.float32)
        odd = jnp.zeros((half, channels), jnp.float32)
        for j in range(half):
            even = even + consts_ref[:, 1 + j : 2 + j] * cosine[j : j + 1, :]
            odd = odd + consts_ref[:, 1 + half + j : 2 + half + j] * sine[j : j + 1, :]
        mid_c, mid_s = sincos_turns(offset * (K_MID / TWO_PI))
        mid_c, mid_s = mid_c * spread, mid_s * spread
        rows = jnp.concatenate([mid_c * even, -mid_s * odd, -mid_s * even, -mid_c * odd], axis=0)
        coef_ref[s] = rows.T.astype(jnp.bfloat16)

    chunk = 512

    def source(s, matched):
        z = depths_ref[s]
        terms = pl.ds(pl.multiple_of(z * (2 * TERMS), 2 * TERMS), 2 * TERMS)
        coef = coef_ref[s]
        total = jnp.zeros((channels, LANES), jnp.float32)
        for start in range(0, samples, chunk):
            series = jnp.dot(
                coef, psi_ref[terms, start : start + chunk], preferred_element_type=jnp.float32
            )
            product = jnp.tanh(series) * recorded_ref[:, start : start + chunk].astype(jnp.float32)
            for tile in range(chunk // LANES):
                total = total + product[:, tile * LANES : (tile + 1) * LANES]
        value = jnp.sum(total, axis=1, keepdims=True)
        lane = lax.broadcasted_iota(jnp.int32, (channels, LANES), 1)
        return jnp.where(lane == s, value, matched)

    out_ref[...] = lax.fori_loop(
        0, sources, source, jnp.zeros((channels, LANES), jnp.float32)
    )


def exchange_kernel(sizes, block_ref, out_ref, held_ref, send_sem, recv_sem):
    freq_size, sub_size = sizes
    count = freq_size * sub_size
    me = lax.axis_index("freq") * sub_size + lax.axis_index("sub")
    barrier = pltpu.get_barrier_semaphore()

    def place(number):
        return {"freq": number // sub_size, "sub": number % sub_size}

    def greet(i, carry):
        pl.semaphore_signal(
            barrier,
            inc=1,
            device_id=place((me + i) % count),
            device_id_type=pl.DeviceIdType.MESH,
        )
        return carry

    lax.fori_loop(1, count, greet, 0)
    pl.semaphore_wait(barrier, count - 1)

    def copy_to(target, source):
        return pltpu.make_async_remote_copy(
            src_ref=block_ref.at[target],
            dst_ref=held_ref.at[source],
            send_sem=send_sem.at[target],
            recv_sem=recv_sem.at[source],
            device_id=place(target),
            device_id_type=pl.DeviceIdType.MESH,
        )

    def send(i, carry):
        copy_to((me + i) % count, me).start()
        return carry

    lax.fori_loop(1, count, send, 0)

    def receive(i, total):
        source = (me + count - i) % count
        copy_to(source, source).wait_recv()
        return total + held_ref[source]

    out_ref[...] = lax.fori_loop(1, count, receive, block_ref[me])

    def drain(i, carry):
        copy_to((me + i) % count, me).wait_send()
        return carry

    lax.fori_loop(1, count, drain, 0)


def per_device(
    mesh_sizes,
    wavenumbers,
    receiver_shapes,
    source_shapes,
    mode_counts,
    source_depths,
    source_ranges,
    sections,
    recorded,
):
    freq_size, sub_size = mesh_sizes
    count = freq_size * sub_size
    me = lax.axis_index("freq") * sub_size + lax.axis_index("sub")
    bins, modes = wavenumbers.shape
    depth_grid = source_shapes.shape[1]
    sources = source_depths.shape[0]
    channels, samples = recorded.shape
    receivers = channels * count
    width = -(-modes // LANES) * LANES

    first_x = 1.0 + 2.0 * (me * channels).astype(jnp.float32) / receivers
    reach = 2.0 * (channels - 1) / receivers
    centre = first_x + 0.5 * (reach - R_TOP)
    top_phase = K_HALF * 0.5 * (reach + R_TOP)
    assert 2.0 * (0.5 * top_phase) ** TERMS / math.factorial(TERMS) < 1e-9
    assert depth_grid * 2 * TERMS <= LANES

    def regroup(value, fill):
        value = jnp.pad(value, [(0, 0)] * (value.ndim - 1) + [(0, width - modes)], constant_values=fill)
        shape = value.shape
        value = value.reshape(shape[:-2] + (bins // 4, 4, width))
        return jnp.swapaxes(value, -3, -2).reshape(shape)

    wave = wavenumbers
    live = jnp.arange(modes, dtype=jnp.int32)[None, :] < mode_counts[:, None]
    factor = receiver_shapes.astype(jnp.float32) * (8.0 / math.sqrt(bins))
    factor = jnp.where(live, factor / jnp.sqrt(wave * modes), 0.0)
    ampl = jnp.swapaxes(source_shapes, 0, 1).astype(jnp.float32) * factor[None]
    ampl = jnp.pad(ampl, ((0, LANES // (2 * TERMS) - depth_grid), (0, 0), (0, 0)))
    shape = (bins, modes, LANES // (2 * TERMS), sources, channels, samples, receivers)
    matched = pl.pallas_call(
        functools.partial(replica_kernel, shape),
        out_shape=jax.ShapeDtypeStruct((channels, LANES), jnp.float32),
        in_specs=[pl.BlockSpec(memory_space=pltpu.SMEM)] * 3
        + [pl.BlockSpec(memory_space=pltpu.VMEM)] * 4,
        out_specs=pl.BlockSpec(memory_space=pltpu.VMEM),
        scratch_shapes=[
            pltpu.VMEM((bins, LANES), jnp.float32),
            pltpu.VMEM((bins, LANES), jnp.float32),
            pltpu.VMEM((bins // 2, samples // 4), jnp.bfloat16),
            pltpu.VMEM((4, LANES, samples // 4), jnp.float32),
            pltpu.VMEM((LANES, samples), jnp.bfloat16),
            pltpu.VMEM((sources, channels, 2 * TERMS), jnp.bfloat16),
        ],
        compiler_params=pltpu.CompilerParams(vmem_limit_bytes=48 * 1024 * 1024),
        name="replica",
    )(
        source_depths,
        jnp.stack([first_x, centre]),
        source_ranges,
        jnp.asarray(term_constants()),
        regroup(wave, K_MID),
        regroup(ampl, 0.0),
        recorded,
    )

    section_count = receivers // 4
    own = section_count // count
    padded = -(-own // 8) * 8
    slot = jnp.arange(count * padded, dtype=jnp.int32)
    wanted = jnp.where(slot % padded < own, slot // padded * own + slot % padded, -1)
    member = (wanted[:, None] == sections[None, :]).astype(jnp.float32)
    blocks = jnp.dot(member, matched, precision=lax.Precision.HIGHEST) * (
        1.0 / math.sqrt(samples * (receivers // section_count))
    )
    blocks = blocks.reshape(count, padded, LANES)
    total = pl.pallas_call(
        functools.partial(exchange_kernel, (freq_size, sub_size)),
        out_shape=jax.ShapeDtypeStruct((padded, LANES), jnp.float32),
        in_specs=[pl.BlockSpec(memory_space=pltpu.VMEM)],
        out_specs=pl.BlockSpec(memory_space=pltpu.VMEM),
        scratch_shapes=[
            pltpu.VMEM((count, padded, LANES), jnp.float32),
            pltpu.SemaphoreType.DMA((count,)),
            pltpu.SemaphoreType.DMA((count,)),
        ],
        compiler_params=pltpu.CompilerParams(collective_id=0, has_side_effects=True),
        name="exchange",
    )(blocks)
    return total[:own, :sources].T


def solution(mesh):
    sizes = (mesh.shape["freq"], mesh.shape["sub"])
    in_specs = (
        P(),
        P(),
        P(),
        P(),
        P("groups"),
        P("groups"),
        P(("freq", "sub")),
        P(("freq", "sub"), None),
    )
    out_specs = P("groups", ("freq", "sub"))
    return jax.shard_map(
        functools.partial(per_device, sizes),
        mesh=mesh,
        in_specs=in_specs,
        out_specs=out_specs,
        check_vma=False,
    )
```

```python
import functools
import math

import jax
import jax.numpy as jnp
import numpy as np
from jax import lax
from jax.experimental import pallas as pl
from jax.experimental.pallas import tpu as pltpu
from jax.sharding import PartitionSpec as P

MMIN = 64
F0 = 256
SPREAD = 16
K_LOW, K_TOP = 1.0, 20.0
R_TOP = 0.5
K_MID, K_HALF = 0.5 * (K_LOW + K_TOP), 0.5 * (K_TOP - K_LOW)
LANES = 128
TERMS = 16
TWO_PI = 2.0 * math.pi


def sincos_turns(turns):
    part = turns - jnp.floor(turns + 0.5)
    sq = part * part
    p2 = math.pi * math.pi
    s = jnp.full_like(part, -(p2**5) / math.factorial(11))
    for n in (9, 7, 5, 3, 1):
        s = s * sq + ((-1) ** ((n - 1) // 2)) * p2 ** ((n - 1) // 2) / math.factorial(n)
    s = s * (part * math.pi)
    c = jnp.full_like(part, p2**6 / math.factorial(12))
    for n in (10, 8, 6, 4, 2, 0):
        c = c * sq + ((-1) ** (n // 2)) * p2 ** (n // 2) / math.factorial(n)
    return 1.0 - 2.0 * s * s, 2.0 * s * c


def term_constants():
    nodes = np.cos(np.pi * (np.arange(TERMS) + 0.5) / TERMS)[: TERMS // 2]
    order = np.arange(TERMS)
    table = np.cos(order[:, None] * np.arccos(nodes)[None, :])
    table *= (np.where(order == 0, 1.0, 2.0) * 2.0 / TERMS)[:, None]
    half = TERMS // 2
    out = np.zeros((half, LANES), np.float32)
    out[:, 0] = K_HALF * nodes
    out[:, 1 : 1 + half] = table[0::2]
    out[:, 1 + half : 1 + 2 * half] = table[1::2]
    return out


def place_of(n):
    return n // 2 if n % 2 == 0 else TERMS // 2 + n // 2


def replica_kernel(
    shape,
    depths_ref,
    place_ref,
    ranges_ref,
    consts_ref,
    wave_ref,
    factor_ref,
    source_ref,
    recorded_ref,
    out_ref,
    sum_ref,
    weight_ref,
    term_ref,
    tab_ref,
    part_ref,
    psi_ref,
    coef_ref,
):
    bins, modes, depth_grid, sources, channels, samples, receivers = shape
    quarter = bins // 4
    span = samples // 4
    half = TERMS // 2
    first_x = place_ref[0]
    centre = place_ref[1]

    for first in range(0, bins, LANES):
        last = first + LANES - 1
        top = min(modes, MMIN + (modes - MMIN) * last // max(bins - 1, 1) + SPREAD)
        cols = slice(first, first + LANES)

        def modal(step, sums, cols=cols):
            start = pl.multiple_of(step * 8, 8)
            rows = pl.ds(start, 8)
            wave = wave_ref[rows, cols]
            cosine, sine = sincos_turns(wave * (centre * (1.0 / TWO_PI)))
            factor = factor_ref[rows, cols]
            weight_ref[0:8, :] = factor * cosine
            weight_ref[8:16, :] = factor * sine
            xi = (wave - K_MID) * (1.0 / K_HALF)
            before, now = jnp.ones_like(xi), xi
            for n in range(1, TERMS):
                term_ref[n * 8 : n * 8 + 8, :] = now
                before, now = now, 2.0 * xi * now - before
            sums = list(sums)
            for i in range(8):
                source = source_ref[jnp.minimum(start + i, modes - 1), :, cols].astype(jnp.float32)
                value = jnp.concatenate(
                    [source * weight_ref[i : i + 1, :], source * weight_ref[8 + i : 9 + i, :]], axis=0
                )
                sums[0] = sums[0] + value
                for n in range(1, TERMS):
                    sums[n] = sums[n] + value * term_ref[n * 8 + i : n * 8 + i + 1, :]
            return tuple(sums)

        zero = jnp.zeros((2 * depth_grid, LANES), jnp.float32)
        sums = lax.fori_loop(0, -(-top // 8), modal, (zero,) * TERMS)
        for n in range(TERMS):
            for z in range(depth_grid):
                for c in range(2):
                    at = z * 2 * TERMS + c * TERMS + place_of(n)
                    row = c * depth_grid + z
                    sum_ref[at : at + 1, cols] = sums[n][row : row + 1, :]

    def times_i(value):
        blocks = []
        for z in range(depth_grid):
            base = z * 2 * TERMS
            blocks.append(-value[base + TERMS : base + 2 * TERMS])
            blocks.append(value[base : base + TERMS])
        return jnp.concatenate(blocks, axis=0)

    moments = sum_ref[...]
    moments = jnp.concatenate([moments, -times_i(moments)], axis=0).astype(jnp.bfloat16)
    group = depth_grid * 2 * TERMS

    for r in range(4):
        row = lax.broadcasted_iota(jnp.int32, (quarter, LANES), 0)
        column = lax.broadcasted_iota(jnp.int32, (quarter, LANES), 1)
        number = F0 + 4 * row + r
        whole = (number * column) % samples
        cosine, sine = sincos_turns(whole.astype(jnp.float32) * (1.0 / samples))
        turn = (number * LANES) % samples
        step_c, step_s = sincos_turns(turn.astype(jnp.float32) * (1.0 / samples))
        for block in range(span // LANES):
            cols = slice(block * LANES, (block + 1) * LANES)
            tab_ref[:quarter, cols] = cosine.astype(jnp.bfloat16)
            tab_ref[quarter:, cols] = (-sine).astype(jnp.bfloat16)
            cosine, sine = cosine * step_c - sine * step_s, cosine * step_s + sine * step_c
        bin_row = lax.broadcasted_iota(jnp.int32, (bins, quarter), 0)
        bin_column = lax.broadcasted_iota(jnp.int32, (bins, quarter), 1)
        chosen = (bin_row == 4 * bin_column + r).astype(jnp.float32).astype(jnp.bfloat16)
        picked = jnp.dot(moments, chosen, preferred_element_type=jnp.float32)
        left = jnp.concatenate([picked[:group], picked[group:]], axis=1)
        part_ref[r] = jnp.dot(
            left.astype(jnp.bfloat16), tab_ref[...], preferred_element_type=jnp.float32
        )

    for block in range(span // LANES):
        cols = slice(block * LANES, (block + 1) * LANES)
        p0, p1, p2, p3 = (part_ref[r, :, cols] for r in range(4))
        even, odd = p0 + p2, p1 + p3
        gap, turned = p0 - p2, times_i(p1 - p3)
        for q, value in enumerate((even + odd, gap + turned, even - odd, gap - turned)):
            at = q * span + block * LANES
            psi_ref[:, at : at + LANES] = value.astype(jnp.bfloat16)

    channel = lax.broadcasted_iota(jnp.int32, (1, channels), 1).astype(jnp.float32)
    position = first_x + channel * (2.0 / receivers)
    spread = lax.rsqrt(position)
    nodes = consts_ref[:, 0:1]
    for s in range(sources):
        offset = position - (ranges_ref[s] + centre)
        cosine, sine = sincos_turns(nodes * offset * (1.0 / TWO_PI))
        even = jnp.zeros((half, channels), jnp.float32)
        odd = jnp.zeros((half, channels), jnp.float32)
        for j in range(half):
            even = even + consts_ref[:, 1 + j : 2 + j] * cosine[j : j + 1, :]
            odd = odd + consts_ref[:, 1 + half + j : 2 + half + j] * sine[j : j + 1, :]
        mid_c, mid_s = sincos_turns(offset * (K_MID / TWO_PI))
        mid_c, mid_s = mid_c * spread, mid_s * spread
        rows = jnp.concatenate([mid_c * even, -mid_s * odd, -mid_s * even, -mid_c * odd], axis=0)
        coef_ref[s] = rows.T.astype(jnp.bfloat16)

    chunk = 512

    def source(s, matched):
        z = depths_ref[s]
        terms = pl.ds(pl.multiple_of(z * (2 * TERMS), 2 * TERMS), 2 * TERMS)
        coef = coef_ref[s]
        total = jnp.zeros((channels, LANES), jnp.float32)
        for start in range(0, samples, chunk):
            series = jnp.dot(
                coef, psi_ref[terms, start : start + chunk], preferred_element_type=jnp.float32
            )
            product = jnp.tanh(series) * recorded_ref[:, start : start + chunk].astype(jnp.float32)
            for tile in range(chunk // LANES):
                total = total + product[:, tile * LANES : (tile + 1) * LANES]
        value = jnp.sum(total, axis=1, keepdims=True)
        lane = lax.broadcasted_iota(jnp.int32, (channels, LANES), 1)
        return jnp.where(lane == s, value, matched)

    out_ref[...] = lax.fori_loop(
        0, sources, source, jnp.zeros((channels, LANES), jnp.float32)
    )


def exchange_kernel(sizes, block_ref, out_ref, held_ref, send_sem, recv_sem):
    freq_size, sub_size = sizes
    count = freq_size * sub_size
    me = lax.axis_index("freq") * sub_size + lax.axis_index("sub")
    barrier = pltpu.get_barrier_semaphore()

    def place(number):
        return {"freq": number // sub_size, "sub": number % sub_size}

    def greet(i, carry):
        pl.semaphore_signal(
            barrier,
            inc=1,
            device_id=place((me + i) % count),
            device_id_type=pl.DeviceIdType.MESH,
        )
        return carry

    lax.fori_loop(1, count, greet, 0)
    pl.semaphore_wait(barrier, count - 1)

    def copy_to(target, source):
        return pltpu.make_async_remote_copy(
            src_ref=block_ref.at[target],
            dst_ref=held_ref.at[source],
            send_sem=send_sem.at[target],
            recv_sem=recv_sem.at[source],
            device_id=place(target),
            device_id_type=pl.DeviceIdType.MESH,
        )

    def send(i, carry):
        copy_to((me + i) % count, me).start()
        return carry

    lax.fori_loop(1, count, send, 0)

    def receive(i, total):
        source = (me + count - i) % count
        copy_to(source, source).wait_recv()
        return total + held_ref[source]

    out_ref[...] = lax.fori_loop(1, count, receive, block_ref[me])

    def drain(i, carry):
        copy_to((me + i) % count, me).wait_send()
        return carry

    lax.fori_loop(1, count, drain, 0)


def per_device(
    mesh_sizes,
    wavenumbers,
    receiver_shapes,
    source_shapes,
    mode_counts,
    source_depths,
    source_ranges,
    sections,
    recorded,
):
    freq_size, sub_size = mesh_sizes
    count = freq_size * sub_size
    me = lax.axis_index("freq") * sub_size + lax.axis_index("sub")
    bins, modes = wavenumbers.shape
    depth_grid = source_shapes.shape[1]
    sources = source_depths.shape[0]
    channels, samples = recorded.shape
    receivers = channels * count

    first_x = 1.0 + 2.0 * (me * channels).astype(jnp.float32) / receivers
    reach = 2.0 * (channels - 1) / receivers
    centre = first_x + 0.5 * (reach - R_TOP)
    top_phase = K_HALF * 0.5 * (reach + R_TOP)
    assert 2.0 * (0.5 * top_phase) ** TERMS / math.factorial(TERMS) < 1e-9
    assert depth_grid * 2 * TERMS <= LANES

    extra = -modes % 8
    wave = wavenumbers.T
    live = jnp.arange(modes, dtype=jnp.int32)[:, None] < mode_counts[None, :]
    factor = receiver_shapes.T.astype(jnp.float32) * (8.0 / math.sqrt(bins))
    factor = jnp.where(live, factor / jnp.sqrt(wave * modes), 0.0)
    factor = jnp.pad(factor, ((0, extra), (0, 0)))
    wave = jnp.pad(wave, ((0, extra), (0, 0)), constant_values=K_MID)
    shape = (bins, modes, depth_grid, sources, channels, samples, receivers)
    matched = pl.pallas_call(
        functools.partial(replica_kernel, shape),
        out_shape=jax.ShapeDtypeStruct((channels, LANES), jnp.float32),
        in_specs=[pl.BlockSpec(memory_space=pltpu.SMEM)] * 3
        + [pl.BlockSpec(memory_space=pltpu.VMEM)] * 5,
        out_specs=pl.BlockSpec(memory_space=pltpu.VMEM),
        scratch_shapes=[
            pltpu.VMEM((depth_grid * 2 * TERMS, bins), jnp.float32),
            pltpu.VMEM((16, LANES), jnp.float32),
            pltpu.VMEM((TERMS * 8, LANES), jnp.float32),
            pltpu.VMEM((bins // 2, samples // 4), jnp.bfloat16),
            pltpu.VMEM((4, depth_grid * 2 * TERMS, samples // 4), jnp.float32),
            pltpu.VMEM((depth_grid * 2 * TERMS, samples), jnp.bfloat16),
            pltpu.VMEM((sources, channels, 2 * TERMS), jnp.bfloat16),
        ],
        compiler_params=pltpu.CompilerParams(vmem_limit_bytes=48 * 1024 * 1024),
        name="replica",
    )(
        source_depths,
        jnp.stack([first_x, centre]),
        source_ranges,
        jnp.asarray(term_constants()),
        wave,
        factor,
        source_shapes.transpose(2, 1, 0),
        recorded,
    )

    section_count = receivers // 4
    own = section_count // count
    padded = -(-own // 8) * 8
    slot = jnp.arange(count * padded, dtype=jnp.int32)
    wanted = jnp.where(slot % padded < own, slot // padded * own + slot % padded, -1)
    member = (wanted[:, None] == sections[None, :]).astype(jnp.float32)
    blocks = jnp.dot(member, matched, precision=lax.Precision.HIGHEST) * (
        1.0 / math.sqrt(samples * (receivers // section_count))
    )
    blocks = blocks.reshape(count, padded, LANES)
    total = pl.pallas_call(
        functools.partial(exchange_kernel, (freq_size, sub_size)),
        out_shape=jax.ShapeDtypeStruct((padded, LANES), jnp.float32),
        in_specs=[pl.BlockSpec(memory_space=pltpu.VMEM)],
        out_specs=pl.BlockSpec(memory_space=pltpu.VMEM),
        scratch_shapes=[
            pltpu.VMEM((count, padded, LANES), jnp.float32),
            pltpu.SemaphoreType.DMA((count,)),
            pltpu.SemaphoreType.DMA((count,)),
        ],
        compiler_params=pltpu.CompilerParams(collective_id=0, has_side_effects=True),
        name="exchange",
    )(blocks)
    return total[:own, :sources].T


def solution(mesh):
    sizes = (mesh.shape["freq"], mesh.shape["sub"])
    in_specs = (
        P(),
        P(),
        P(),
        P(),
        P("groups"),
        P("groups"),
        P(("freq", "sub")),
        P(("freq", "sub"), None),
    )
    out_specs = P("groups", ("freq", "sub"))
    return jax.shard_map(
        functools.partial(per_device, sizes),
        mesh=mesh,
        in_specs=in_specs,
        out_specs=out_specs,
        check_vma=False,
    )
```

```python
import functools
import math

import jax
import jax.numpy as jnp
import numpy as np
from jax import lax
from jax.experimental import pallas as pl
from jax.experimental.pallas import tpu as pltpu
from jax.sharding import PartitionSpec as P

MMIN = 64
F0 = 256
SPREAD = 16
K_LOW, K_TOP = 1.0, 20.0
R_TOP = 0.5
K_MID, K_HALF = 0.5 * (K_LOW + K_TOP), 0.5 * (K_TOP - K_LOW)
LANES = 128
TERMS = 16
TWO_PI = 2.0 * math.pi


def sincos_turns(turns):
    part = turns - jnp.floor(turns + 0.5)
    sq = part * part
    p2 = math.pi * math.pi
    s = jnp.full_like(part, -(p2**5) / math.factorial(11))
    for n in (9, 7, 5, 3, 1):
        s = s * sq + ((-1) ** ((n - 1) // 2)) * p2 ** ((n - 1) // 2) / math.factorial(n)
    s = s * (part * math.pi)
    c = jnp.full_like(part, p2**6 / math.factorial(12))
    for n in (10, 8, 6, 4, 2, 0):
        c = c * sq + ((-1) ** (n // 2)) * p2 ** (n // 2) / math.factorial(n)
    return 1.0 - 2.0 * s * s, 2.0 * s * c


def term_constants():
    nodes = np.cos(np.pi * (np.arange(TERMS) + 0.5) / TERMS)[: TERMS // 2]
    order = np.arange(TERMS)
    table = np.cos(order[:, None] * np.arccos(nodes)[None, :])
    table *= (np.where(order == 0, 1.0, 2.0) * 2.0 / TERMS)[:, None]
    half = TERMS // 2
    out = np.zeros((half, LANES), np.float32)
    out[:, 0] = K_HALF * nodes
    out[:, 1 : 1 + half] = table[0::2]
    out[:, 1 + half : 1 + 2 * half] = table[1::2]
    return out


def place_of(n):
    return n // 2 if n % 2 == 0 else TERMS // 2 + n // 2


def replica_kernel(
    shape,
    depths_ref,
    place_ref,
    ranges_ref,
    consts_ref,
    wave_ref,
    factor_ref,
    source_ref,
    recorded_ref,
    out_ref,
    sum_ref,
    weight_ref,
    term_ref,
    tab_ref,
    part_ref,
    psi_ref,
    coef_ref,
):
    bins, modes, depth_grid, sources, channels, samples, receivers = shape
    quarter = bins // 4
    span = samples // 4
    half = TERMS // 2
    first_x = place_ref[0]
    centre = place_ref[1]

    for first in range(0, bins, LANES):
        last = first + LANES - 1
        top = min(modes, MMIN + (modes - MMIN) * last // max(bins - 1, 1) + SPREAD)
        cols = slice(first, first + LANES)

        def modal(step, sums, cols=cols):
            start = pl.multiple_of(step * 8, 8)
            rows = pl.ds(start, 8)
            wave = wave_ref[rows, cols]
            cosine, sine = sincos_turns(wave * (centre * (1.0 / TWO_PI)))
            factor = factor_ref[rows, cols]
            weight_ref[0:8, :] = factor * cosine
            weight_ref[8:16, :] = factor * sine
            xi = (wave - K_MID) * (1.0 / K_HALF)
            before, now = jnp.ones_like(xi), xi
            for n in range(1, TERMS):
                term_ref[n * 8 : n * 8 + 8, :] = now
                before, now = now, 2.0 * xi * now - before
            sums = list(sums)
            for i in range(8):
                source = source_ref[jnp.minimum(start + i, modes - 1), :, cols].astype(jnp.float32)
                value = jnp.concatenate(
                    [source * weight_ref[i : i + 1, :], source * weight_ref[8 + i : 9 + i, :]], axis=0
                )
                sums[0] = sums[0] + value
                for n in range(1, TERMS):
                    sums[n] = sums[n] + value * term_ref[n * 8 + i : n * 8 + i + 1, :]
            return tuple(sums)

        zero = jnp.zeros((2 * depth_grid, LANES), jnp.float32)
        sums = lax.fori_loop(0, -(-top // 8), modal, (zero,) * TERMS)
        for n in range(TERMS):
            for z in range(depth_grid):
                for c in range(2):
                    at = z * 2 * TERMS + c * TERMS + place_of(n)
                    row = c * depth_grid + z
                    sum_ref[at : at + 1, cols] = sums[n][row : row + 1, :]

    def times_i(value):
        blocks = []
        for z in range(depth_grid):
            base = z * 2 * TERMS
            blocks.append(-value[base + TERMS : base + 2 * TERMS])
            blocks.append(value[base : base + TERMS])
        return jnp.concatenate(blocks, axis=0)

    moments = sum_ref[...]
    moments = jnp.concatenate([moments, -times_i(moments)], axis=0).astype(jnp.bfloat16)
    group = depth_grid * 2 * TERMS

    for r in range(4):
        row = lax.broadcasted_iota(jnp.int32, (quarter, LANES), 0)
        column = lax.broadcasted_iota(jnp.int32, (quarter, LANES), 1)
        number = F0 + 4 * row + r
        whole = (number * column) % samples
        cosine, sine = sincos_turns(whole.astype(jnp.float32) * (1.0 / samples))
        turn = (number * LANES) % samples
        step_c, step_s = sincos_turns(turn.astype(jnp.float32) * (1.0 / samples))
        for block in range(span // LANES):
            cols = slice(block * LANES, (block + 1) * LANES)
            tab_ref[:quarter, cols] = cosine.astype(jnp.bfloat16)
            tab_ref[quarter:, cols] = (-sine).astype(jnp.bfloat16)
            cosine, sine = cosine * step_c - sine * step_s, cosine * step_s + sine * step_c
        bin_row = lax.broadcasted_iota(jnp.int32, (bins, quarter), 0)
        bin_column = lax.broadcasted_iota(jnp.int32, (bins, quarter), 1)
        chosen = (bin_row == 4 * bin_column + r).astype(jnp.float32).astype(jnp.bfloat16)
        picked = jnp.dot(moments, chosen, preferred_element_type=jnp.float32)
        left = jnp.concatenate([picked[:group], picked[group:]], axis=1)
        part_ref[r] = jnp.dot(
            left.astype(jnp.bfloat16), tab_ref[...], preferred_element_type=jnp.float32
        )

    for block in range(span // LANES):
        cols = slice(block * LANES, (block + 1) * LANES)
        p0, p1, p2, p3 = (part_ref[r, :, cols] for r in range(4))
        even, odd = p0 + p2, p1 + p3
        gap, turned = p0 - p2, times_i(p1 - p3)
        for q, value in enumerate((even + odd, gap + turned, even - odd, gap - turned)):
            at = q * span + block * LANES
            psi_ref[:, at : at + LANES] = value.astype(jnp.bfloat16)

    channel = lax.broadcasted_iota(jnp.int32, (1, channels), 1).astype(jnp.float32)
    position = first_x + channel * (2.0 / receivers)
    spread = lax.rsqrt(position)
    nodes = consts_ref[:, 0:1]
    for s in range(sources):
        offset = position - (ranges_ref[s] + centre)
        cosine, sine = sincos_turns(nodes * offset * (1.0 / TWO_PI))
        even = jnp.zeros((half, channels), jnp.float32)
        odd = jnp.zeros((half, channels), jnp.float32)
        for j in range(half):
            even = even + consts_ref[:, 1 + j : 2 + j] * cosine[j : j + 1, :]
            odd = odd + consts_ref[:, 1 + half + j : 2 + half + j] * sine[j : j + 1, :]
        mid_c, mid_s = sincos_turns(offset * (K_MID / TWO_PI))
        mid_c, mid_s = mid_c * spread, mid_s * spread
        rows = jnp.concatenate([mid_c * even, -mid_s * odd, -mid_s * even, -mid_c * odd], axis=0)
        coef_ref[s] = rows.T.astype(jnp.bfloat16)

    chunk = 512

    def source(s, matched):
        z = depths_ref[s]
        terms = pl.ds(pl.multiple_of(z * (2 * TERMS), 2 * TERMS), 2 * TERMS)
        coef = coef_ref[s]
        total = jnp.zeros((channels, LANES), jnp.float32)
        for start in range(0, samples, chunk):
            series = jnp.dot(
                coef, psi_ref[terms, start : start + chunk], preferred_element_type=jnp.float32
            )
            product = jnp.tanh(series) * recorded_ref[:, start : start + chunk].astype(jnp.float32)
            for tile in range(chunk // LANES):
                total = total + product[:, tile * LANES : (tile + 1) * LANES]
        value = jnp.sum(total, axis=1, keepdims=True)
        lane = lax.broadcasted_iota(jnp.int32, (channels, LANES), 1)
        return jnp.where(lane % sources == s, value, matched)

    out_ref[...] = lax.fori_loop(
        0, sources, source, jnp.zeros((channels, LANES), jnp.float32)
    )


def exchange_kernel(sizes, block_ref, out_ref, held_ref, send_sem, recv_sem):
    freq_size, sub_size = sizes
    count = freq_size * sub_size
    me = lax.axis_index("freq") * sub_size + lax.axis_index("sub")
    barrier = pltpu.get_barrier_semaphore()

    def place(number):
        return {"freq": number // sub_size, "sub": number % sub_size}

    def greet(i, carry):
        pl.semaphore_signal(
            barrier,
            inc=1,
            device_id=place((me + i) % count),
            device_id_type=pl.DeviceIdType.MESH,
        )
        return carry

    lax.fori_loop(1, count, greet, 0)
    pl.semaphore_wait(barrier, count - 1)

    def copy_to(target, source):
        return pltpu.make_async_remote_copy(
            src_ref=block_ref.at[target],
            dst_ref=held_ref.at[source],
            send_sem=send_sem.at[target],
            recv_sem=recv_sem.at[source],
            device_id=place(target),
            device_id_type=pl.DeviceIdType.MESH,
        )

    def send(i, carry):
        copy_to((me + i) % count, me).start()
        return carry

    lax.fori_loop(1, count, send, 0)

    def receive(i, total):
        source = (me + count - i) % count
        copy_to(source, source).wait_recv()
        return total + held_ref[source]

    out_ref[...] = lax.fori_loop(1, count, receive, block_ref[me])

    def drain(i, carry):
        copy_to((me + i) % count, me).wait_send()
        return carry

    lax.fori_loop(1, count, drain, 0)


def per_device(
    mesh_sizes,
    wavenumbers,
    receiver_shapes,
    source_shapes,
    mode_counts,
    source_depths,
    source_ranges,
    sections,
    recorded,
):
    freq_size, sub_size = mesh_sizes
    count = freq_size * sub_size
    me = lax.axis_index("freq") * sub_size + lax.axis_index("sub")
    bins, modes = wavenumbers.shape
    depth_grid = source_shapes.shape[1]
    sources = source_depths.shape[0]
    channels, samples = recorded.shape
    receivers = channels * count

    first_x = 1.0 + 2.0 * (me * channels).astype(jnp.float32) / receivers
    reach = 2.0 * (channels - 1) / receivers
    centre = first_x + 0.5 * (reach - R_TOP)
    top_phase = K_HALF * 0.5 * (reach + R_TOP)
    assert 2.0 * (0.5 * top_phase) ** TERMS / math.factorial(TERMS) < 1e-9
    assert depth_grid * 2 * TERMS <= LANES

    extra = -modes % 8
    wave = wavenumbers.T
    live = jnp.arange(modes, dtype=jnp.int32)[:, None] < mode_counts[None, :]
    factor = receiver_shapes.T.astype(jnp.float32) * (8.0 / math.sqrt(bins))
    factor = jnp.where(live, factor / jnp.sqrt(wave * modes), 0.0)
    factor = jnp.pad(factor, ((0, extra), (0, 0)))
    wave = jnp.pad(wave, ((0, extra), (0, 0)), constant_values=K_MID)
    shape = (bins, modes, depth_grid, sources, channels, samples, receivers)
    matched = pl.pallas_call(
        functools.partial(replica_kernel, shape),
        out_shape=jax.ShapeDtypeStruct((channels, LANES), jnp.float32),
        in_specs=[pl.BlockSpec(memory_space=pltpu.SMEM)] * 3
        + [pl.BlockSpec(memory_space=pltpu.VMEM)] * 5,
        out_specs=pl.BlockSpec(memory_space=pltpu.VMEM),
        scratch_shapes=[
            pltpu.VMEM((depth_grid * 2 * TERMS, bins), jnp.float32),
            pltpu.VMEM((16, LANES), jnp.float32),
            pltpu.VMEM((TERMS * 8, LANES), jnp.float32),
            pltpu.VMEM((bins // 2, samples // 4), jnp.bfloat16),
            pltpu.VMEM((4, depth_grid * 2 * TERMS, samples // 4), jnp.float32),
            pltpu.VMEM((depth_grid * 2 * TERMS, samples), jnp.bfloat16),
            pltpu.VMEM((sources, channels, 2 * TERMS), jnp.bfloat16),
        ],
        compiler_params=pltpu.CompilerParams(vmem_limit_bytes=48 * 1024 * 1024),
        name="replica",
    )(
        source_depths,
        jnp.stack([first_x, centre]),
        source_ranges,
        jnp.asarray(term_constants()),
        wave,
        factor,
        source_shapes.transpose(2, 1, 0),
        recorded,
    )

    section_count = receivers // 4
    own = section_count // count
    per_row = min(LANES // sources, own)
    own_rows = own // per_row
    assert LANES % sources == 0 and own % per_row == 0
    padded = -(-own_rows // 8) * 8
    slot = jnp.arange(count * padded, dtype=jnp.int32)
    wanted = jnp.where(
        slot % padded < own_rows, slot // padded * own_rows + slot % padded, -1
    )
    member = (wanted[:, None] == (sections // per_row)[None, :]).astype(jnp.float32)
    lane_part = jnp.arange(LANES, dtype=jnp.int32) // sources
    kept = jnp.where((sections % per_row)[:, None] == lane_part[None, :], matched, 0.0)
    blocks = jnp.dot(member, kept, precision=lax.Precision.HIGHEST) * (
        1.0 / math.sqrt(samples * (receivers // section_count))
    )
    blocks = blocks.reshape(count, padded, LANES)
    total = pl.pallas_call(
        functools.partial(exchange_kernel, (freq_size, sub_size)),
        out_shape=jax.ShapeDtypeStruct((padded, LANES), jnp.float32),
        in_specs=[pl.BlockSpec(memory_space=pltpu.VMEM)],
        out_specs=pl.BlockSpec(memory_space=pltpu.VMEM),
        scratch_shapes=[
            pltpu.VMEM((count, padded, LANES), jnp.float32),
            pltpu.SemaphoreType.DMA((count,)),
            pltpu.SemaphoreType.DMA((count,)),
        ],
        compiler_params=pltpu.CompilerParams(collective_id=0, has_side_effects=True),
        name="exchange",
    )(blocks)
    total = total[:own_rows, : per_row * sources].reshape(own_rows, per_row, sources)
    return total.transpose(2, 0, 1).reshape(sources, own)


def solution(mesh):
    sizes = (mesh.shape["freq"], mesh.shape["sub"])
    in_specs = (
        P(),
        P(),
        P(),
        P(),
        P("groups"),
        P("groups"),
        P(("freq", "sub")),
        P(("freq", "sub"), None),
    )
    out_specs = P("groups", ("freq", "sub"))
    return jax.shard_map(
        functools.partial(per_device, sizes),
        mesh=mesh,
        in_specs=in_specs,
        out_specs=out_specs,
        check_vma=False,
    )
```
